128 devices in a mesh: mom: 4 (over y), tm: 4 (over z_lo, core), pt: 8 (over x, z_hi).
Axes of the slice: x: 4, y: 4, z: 4 (z_hi: 2, z_lo: 2; z = z_hi * 2 + z_lo), core: 2. Of those that a mesh axis runs over, the one named last changes fastest.
Arguments:
- chi_time: bfloat16 [16, 8, 896, 896], P('tm', 'mom', 'pt'), may hold values from -4 to 4
- green: bfloat16 [8, 16, 896, 896], P('mom', 'tm', 'pt'), may hold values from -6 to 6
- band_coeffs: bfloat16 [896, 1024], replicated, may hold values from -1 to 1
Outputs:
- self_energy: float32 [8, 16, 1024], P('mom', 'tm', 'pt')
The draws below stay inside these ranges and needn't reach their ends.
All inputs are finite; a program needn't handle non-finite values.
Results may differ from the reference program's by a relative error of at most 0.009.
Values may be sent and summed in bfloat16 or wider, within the bound.
No kernel may reach another device: no remote copies, remote signals or barrier semaphores. Data moves between devices by JAX's collectives and lax.ppermute only.
A program may use at most 64 MiB of HBM per device.

```python
import math
import jax
import jax.numpy as jnp
from jax import lax

NK = 8
NT = 16
NP = 896
NB = 1024
ORDER = 8


def draw_chi_time(key, part):
    shape = (NT, NK, NP, NP)
    values = jnp.clip(jax.random.normal(key, shape, jnp.float32), -4.0, 4.0)
    return values.astype(jnp.bfloat16)


def block_scale(key, extent, cuts, low, largest):
    level, own = 1.0, jax.random.fold_in(key, 6)
    for position, parts in cuts:
        draws = jnp.exp(jax.random.uniform(jax.random.fold_in(own, position), (parts,), jnp.float32, low / len(cuts), largest / len(cuts)))
        level = level * jnp.repeat(draws, extent[position] // parts).reshape([-1 if axis == position else 1 for axis in range(len(extent))])
    return level


def bell_draw(key, shape, deviation, bound, pieces=(), kind=jnp.bfloat16):
    entries = deviation * jax.random.normal(key, shape, jnp.float32)
    if pieces:
        entries = entries * block_scale(key, shape, pieces, -0.22, 0.18)
    return jnp.clip(entries, -bound, bound).astype(kind)


def setup_inputs(seed: int = 0) -> dict:
    keys = jax.random.split(jax.random.key(seed), 4)
    return {
        "chi_time": draw_chi_time(jax.random.fold_in(keys[3], 71), 0),
        "green": bell_draw(keys[1], (NK, NT, NP, NP), 1.0, 6.0, ((0, 4), (1, 4), (2, 8))),
        "band_coeffs": bell_draw(keys[2], (NP, NB), 28 ** -0.5, 1.0),
    }


COUPLING = 0.8

def cosine_table(count):
    index = jnp.arange(count, dtype=jnp.float32) + 0.5
    angle = jnp.pi * index[:, None] * index[None, :] / count
    return (jnp.sqrt(jnp.float32(2.0 / count)) * jnp.cos(angle)).astype(jnp.bfloat16)

def hartley_table(count):
    index = jnp.arange(count, dtype=jnp.float32)
    angle = 2.0 * jnp.pi * index[:, None] * index[None, :] / count
    return (jnp.cos(angle) + jnp.sin(angle)) / jnp.sqrt(jnp.float32(count))

def series_tile(tile):
    power = tile
    total = tile.astype(jnp.float32)
    for term in range(ORDER - 1):
        power = jnp.dot(power, tile, preferred_element_type=jnp.float32).astype(jnp.bfloat16)
        total = total + power.astype(jnp.float32)
    return total.astype(jnp.bfloat16)

def reference(chi_time, green, band_coeffs):
    highest = lax.Precision.HIGHEST
    cosine = cosine_table(NT).astype(jnp.float32)
    hartley = hartley_table(NK)
    scale = COUPLING / math.sqrt(NP)
    freq = jnp.einsum('wt,tkpq->wkpq', cosine, chi_time.astype(jnp.float32), precision=highest)
    freq = (scale * freq).astype(jnp.bfloat16)
    screened = lax.map(series_tile, freq.reshape(NT * NK, NP, NP)).reshape(NT, NK, NP, NP)
    timed = jnp.einsum('tw,wkpq->tkpq', cosine, screened.astype(jnp.float32), precision=highest)
    lattice = jnp.einsum('rk,tkpq->rtpq', hartley, timed, precision=highest)
    sigma = (green.astype(jnp.float32) * lattice).astype(jnp.bfloat16)
    coeffs = band_coeffs.astype(jnp.float32)

    def project(tile):
        applied = jnp.dot(tile, band_coeffs, preferred_element_type=jnp.float32)
        return lax.optimization_barrier(jnp.sum(coeffs * applied, axis=0))
    values = lax.map(project, sigma.reshape(NK * NT, NP, NP))
    return values.reshape(NK, NT, NB)
```

```python
import math

import jax
import jax.numpy as jnp
import numpy as np
from jax import lax
from jax.experimental import pallas as pl
from jax.experimental.pallas import tpu as pltpu
from jax.sharding import Mesh
from jax.sharding import PartitionSpec as P

COUPLING = 0.8
NT, NK, NP, NB = 16, 8, 896, 1024
GROUPS = 14

C5 = (math.sqrt(22.0) - 1.0) / 4.0
C3 = 0.75 - C5
C4 = 0.625
C6 = 2.0 - 1.25 * C5

TM = ("zlo", "core")
PLANE = ("x", "zhi", "zlo")
BY_ROWS = ("x", "zhi", "mom", "zlo", "core")
BY_OUTPUT = ("mom", "zlo", "core", "x", "zhi")


def exchange(pieces, axes):
    return lax.all_to_all(pieces, axes, split_axis=0, concat_axis=0, tiled=True)


def cosine_table(count):
    index = jnp.arange(count, dtype=jnp.float32) + 0.5
    angle = jnp.pi * index[:, None] * index[None, :] / count
    return (jnp.sqrt(jnp.float32(2.0 / count)) * jnp.cos(angle)).astype(jnp.bfloat16)


def to_frequency(cosine):
    eye = jnp.eye(8, dtype=jnp.bfloat16)
    return jnp.einsum("wt,ab->watb", cosine, eye).reshape(NT * 8, NT * 8)


def to_time(cosine):
    eye = jnp.eye(8, dtype=jnp.bfloat16)
    pair = jnp.eye(2, dtype=jnp.bfloat16)
    return jnp.einsum("tw,cd,ab->ctawdb", cosine, pair, eye).reshape(2 * NT * 8, NT * 2 * 8)


def frequency_kernel(times_ref, table_ref, out_ref):
    table = table_ref[...]
    scale = COUPLING / math.sqrt(NP)
    for group in range(7):
        rows = jnp.concatenate([times_ref[source, group] for source in range(4)], axis=0)
        mixed = jnp.dot(table, rows, preferred_element_type=jnp.float32) * scale
        out_ref[:, 8 * group : 8 * group + 8, :] = mixed.reshape(NT, 8, NP).astype(jnp.bfloat16)


def hartley8(x):
    root = math.sqrt(2.0)
    a0, a1, a2, a3 = x[0] + x[4], x[1] + x[5], x[2] + x[6], x[3] + x[7]
    b0, b1, b2, b3 = x[0] - x[4], x[1] - x[5], x[2] - x[6], x[3] - x[7]
    c0, c1, d0, d1 = a0 + a2, a1 + a3, a0 - a2, a1 - a3
    e0, e1, f1, f3 = b0 + b2, b0 - b2, root * b1, root * b3
    return [c0 + c1, e0 + f1, d0 + d1, e1 + f3, c0 - c1, e0 - f1, d0 - d1, e1 - f3]


def self_energy_kernel(screened_ref, table_ref, green_ref, coeffs_ref, own_ref, out_ref, time_ref, sigma_ref):
    table = table_ref[...]
    for mom in range(4):
        rows = jnp.concatenate([screened_ref[128 * p + 32 * mom : 128 * p + 32 * mom + 32, :] for p in range(8)], axis=0)
        time_ref[mom] = jnp.dot(table, rows, preferred_element_type=jnp.float32)
    norm = 1.0 / math.sqrt(NK)
    for pair in range(NT // 2):
        tiles = [time_ref[k // 2, 128 * (k % 2) + 16 * pair : 128 * (k % 2) + 16 * pair + 16, :] * norm for k in range(NK)]
        cells = hartley8(tiles)
        for r in range(NK):
            at = 256 * (r // 2) + 64 * (pair // 2) + 32 * (r % 2) + 16 * (pair % 2)
            value = green_ref[at : at + 16, :].astype(jnp.float32) * cells[r]
            sigma_ref[at : at + 16, :] = value.astype(jnp.bfloat16)
    own = own_ref[...].astype(jnp.float32)
    for block in range(4):
        applied = jnp.dot(sigma_ref[256 * block : 256 * block + 256, :], coeffs_ref[...], preferred_element_type=jnp.float32)
        values = jnp.sum(applied.reshape(32, 8, NB) * own[None], axis=1)
        for part in range(4):
            for p in range(8):
                out_ref[4 * block + part, p] = values[8 * part : 8 * part + 8, 128 * p : 128 * p + 128]


def local(chi_time, green, band_coeffs):
    cosine = cosine_table(NT)
    params = pltpu.CompilerParams(vmem_limit_bytes=40 * 1024 * 1024)

    e = (lax.axis_index("mom") * 2 + lax.axis_index("zlo")) * 2 + lax.axis_index("core")
    grouped = green.reshape(8, GROUPS, 8, NP).transpose(1, 0, 2, 3)
    grouped = jnp.concatenate([grouped, jnp.zeros((2, 8, 8, NP), jnp.bfloat16)], axis=0)
    cells = exchange(grouped, ("mom", "zlo", "core")).reshape(1024, NP)

    pieces = chi_time.reshape(4, 2, 2, 7, 8, NP).transpose(2, 1, 3, 0, 4, 5).reshape(4, 7, 32, NP)
    times = exchange(pieces, TM)
    mixed = pl.pallas_call(
        frequency_kernel, out_shape=jax.ShapeDtypeStruct((NT, 56, NP), jnp.bfloat16), compiler_params=params
    )(times, to_frequency(cosine))
    tile = exchange(mixed, PLANE).reshape(NP, NP)

    square = jnp.dot(tile, tile, preferred_element_type=jnp.float32).astype(jnp.bfloat16)
    wide, wide2 = tile.astype(jnp.float32), square.astype(jnp.float32)
    fourth = jnp.dot(square, (wide2 + 0.5 * wide).astype(jnp.bfloat16), preferred_element_type=jnp.float32)
    left = (fourth + C3 * wide2 + C4 * wide).astype(jnp.bfloat16)
    right = (fourth + C5 * wide2).astype(jnp.bfloat16)
    total = jnp.dot(left, right, preferred_element_type=jnp.float32) + C6 * fourth + wide2 + wide
    screened = total.astype(jnp.bfloat16).reshape(8, 112, NP)
    screened = jnp.concatenate([screened, jnp.zeros((8, 16, NP), jnp.bfloat16)], axis=1).reshape(128, 8, NP)
    spread = exchange(screened, BY_ROWS).reshape(1024, NP)

    row = (lax.axis_index("x") * 2 + lax.axis_index("zhi")) * 112 + 8 * e
    own = lax.dynamic_slice_in_dim(band_coeffs, row, 8, 0)
    partial_sums = pl.pallas_call(
        self_energy_kernel,
        out_shape=jax.ShapeDtypeStruct((16, 8, 8, 128), jnp.float32),
        scratch_shapes=[pltpu.VMEM((4, 256, NP), jnp.float32), pltpu.VMEM((1024, NP), jnp.bfloat16)],
        compiler_params=params,
    )(spread, to_time(cosine), cells, band_coeffs, own)
    shares = exchange(partial_sums.reshape(128, 8, 128), BY_OUTPUT)
    return shares.sum(axis=0).reshape(2, 4, 128)


def solution(mesh):
    fine = Mesh(mesh.devices.reshape(4, 2, 2, 4, 2), ("mom", "zlo", "core", "x", "zhi"))
    placed = (P(TM, "mom", ("x", "zhi"), None), P("mom", TM, ("x", "zhi"), None), P())
    return jax.shard_map(
        local, mesh=fine, in_specs=placed, out_specs=P("mom", TM, ("x", "zhi")), check_vma=False
    )
```

```python
import math

import jax
import jax.numpy as jnp
import ml_dtypes
import numpy as np
from jax import lax
from jax.experimental import pallas as pl
from jax.experimental.pallas import tpu as pltpu
from jax.sharding import Mesh
from jax.sharding import PartitionSpec as P

COUPLING = 0.8
NT, NK, NP, NB = 16, 8, 896, 1024
GROUPS = 14

C5 = (math.sqrt(22.0) - 1.0) / 4.0
C3 = 0.75 - C5
C4 = 0.625
C6 = 2.0 - 1.25 * C5

TM = ("zlo", "core")
PLANE = ("x", "zhi", "zlo")
BY_ROWS = ("x", "zhi", "mom", "zlo", "core")
BY_OUTPUT = ("mom", "zlo", "core", "x", "zhi")
MIB = 1024 * 1024


def exchange(pieces, axes):
    return lax.all_to_all(pieces, axes, split_axis=0, concat_axis=0, tiled=True)


def swap(piece, axes, step):
    return lax.ppermute(piece, axes, [(i, i ^ step) for i in range(4)])


def mixing_tables():
    index = np.arange(NT) + 0.5
    cosine = (np.sqrt(2.0 / NT) * np.cos(np.pi * index[:, None] * index[None, :] / NT)).astype(np.float32)
    wide, narrow, back = [], [], []
    for tm in range(4):
        times = [4 * ((place // 4) ^ tm) + place % 4 for place in range(NT)]
        wide.append(np.kron(cosine[:, times], np.eye(16)))
        narrow.append(np.kron(cosine[:, times], np.eye(8)))
        back.append(np.einsum("tw,cd,ab->ctawdb", cosine[times, :], np.eye(2), np.eye(8)).reshape(256, 256))
    return [np.stack(tables).astype(ml_dtypes.bfloat16) for tables in (wide, narrow, back)]


def frequency_kernel(own_ref, first_ref, second_ref, third_ref, wide_ref, narrow_ref, out_ref, mixed_ref, sent):
    pieces = (own_ref, first_ref, second_ref, third_ref)
    scale = COUPLING / math.sqrt(NP)
    sends = []

    def send(at, count):
        rows = pl.ds(at, count)
        sends.append(pltpu.make_async_copy(mixed_ref.at[:, rows], out_ref.at[:, rows], sent.at[len(sends)]))
        sends[-1].start()

    rows = jnp.concatenate([piece[t, 48:56, :].astype(jnp.float32) for piece in pieces for t in range(4)], axis=0)
    mixed = jnp.dot(narrow_ref[...], rows.astype(jnp.bfloat16), preferred_element_type=jnp.float32) * scale
    mixed_ref[:, 48:56, :] = mixed.reshape(NT, 8, NP).astype(jnp.bfloat16)
    send(48, 8)
    for at in range(0, 48, 16):
        rows = jnp.concatenate([piece[t, at : at + 16, :] for piece in pieces for t in range(4)], axis=0)
        mixed = jnp.dot(wide_ref[...], rows, preferred_element_type=jnp.float32) * scale
        mixed_ref[:, at : at + 16, :] = mixed.reshape(NT, 16, NP).astype(jnp.bfloat16)
        send(at, 16)
    for move in sends:
        move.wait()


def series_kernel(tile_ref, out_ref, square_ref, sum_ref, fourth_ref, left_ref, right_ref, padded_ref, sent):
    step = 224
    for at in range(0, NP, step):
        rows = slice(at, at + step)
        square = jnp.dot(tile_ref[rows, :], tile_ref[...], preferred_element_type=jnp.float32).astype(jnp.bfloat16)
        square_ref[rows, :] = square
        sum_ref[rows, :] = (square.astype(jnp.float32) + 0.5 * tile_ref[rows, :].astype(jnp.float32)).astype(jnp.bfloat16)
    for at in range(0, NP, step):
        rows = slice(at, at + step)
        fourth = jnp.dot(square_ref[rows, :], sum_ref[...], preferred_element_type=jnp.float32)
        square = square_ref[rows, :].astype(jnp.float32)
        tile = tile_ref[rows, :].astype(jnp.float32)
        left_ref[rows, :] = (fourth + C3 * square + C4 * tile).astype(jnp.bfloat16)
        right_ref[rows, :] = (fourth + C5 * square).astype(jnp.bfloat16)
        fourth_ref[rows, :] = C6 * fourth + square + tile
    for at in range(0, NP, step):
        rows = slice(at, at + step)
        total = jnp.dot(left_ref[rows, :], right_ref[...], preferred_element_type=jnp.float32) + fourth_ref[rows, :]
        total = total.astype(jnp.bfloat16)
        for half in range(2):
            to = 128 * (at // 112 + half)
            padded_ref[to : to + 96, :] = total[112 * half : 112 * half + 96]
            padded_ref[to + 96 : to + 112, :] = jnp.zeros((16, NP), jnp.bfloat16)
            padded_ref[to + 112 : to + 128, :] = total[112 * half + 96 : 112 * half + 112]
        rows = pl.ds(256 * (at // step), 256)
        pltpu.make_async_copy(padded_ref.at[rows], out_ref.at[rows], sent.at[at // step]).start()
    for block in range(4):
        rows = pl.ds(256 * block, 256)
        pltpu.make_async_copy(padded_ref.at[rows], out_ref.at[rows], sent.at[block]).wait()


def hartley8(x):
    root = math.sqrt(2.0)
    a0, a1, a2, a3 = x[0] + x[4], x[1] + x[5], x[2] + x[6], x[3] + x[7]
    b0, b1, b2, b3 = x[0] - x[4], x[1] - x[5], x[2] - x[6], x[3] - x[7]
    c0, c1, d0, d1 = a0 + a2, a1 + a3, a0 - a2, a1 - a3
    e0, e1, f1, f3 = b0 + b2, b0 - b2, root * b1, root * b3
    return [c0 + c1, e0 + f1, d0 + d1, e1 + f3, c0 - c1, e0 - f1, d0 - d1, e1 - f3]


def self_energy_kernel(place_ref, screened_ref, table_ref, *refs):
    cell_refs, (coeffs_ref, _, out_ref, time_ref, sigma_ref) = refs[:4], refs[4:]
    mom_here, tm_here = place_ref[0], place_ref[1]
    table = table_ref[...]
    for mom in range(4):
        rows = jnp.concatenate([screened_ref[128 * p + 32 * mom : 128 * p + 32 * mom + 32, :] for p in range(8)], axis=0)
        time_ref[mom] = jnp.dot(table, rows, preferred_element_type=jnp.float32)
    norm = 1.0 / math.sqrt(NK)
    own = coeffs_ref[NP:, :].astype(jnp.float32)
    for step in range(4):
        for pair in range(2):
            at = 32 * step + 16 * pair
            tiles = [time_ref[k // 2, 128 * (k % 2) + at : 128 * (k % 2) + at + 16, :] * norm for k in range(NK)]
            cells = hartley8(tiles)
            for r in range(NK):
                at = 32 * (r % 2) + 16 * pair
                value = cell_refs[step][(r // 2) ^ mom_here, at : at + 16, :].astype(jnp.float32) * cells[r]
                sigma_ref[step, 64 * (r // 2) + at : 64 * (r // 2) + at + 16, :] = value.astype(jnp.bfloat16)
        applied = jnp.dot(sigma_ref[step], coeffs_ref[:NP, :], preferred_element_type=jnp.float32)
        values = jnp.sum(applied.reshape(32, 8, NB) * own[None], axis=1)
        for mom in range(4):
            for p in range(8):
                share = values[8 * mom : 8 * mom + 8, 128 * p : 128 * p + 128]
                out_ref[4 * mom + (tm_here ^ step), p] = share.astype(out_ref.dtype)


def start_all(copies, done):
    moves = [pltpu.make_async_copy(source, target, done.at[i]) for i, (source, target) in enumerate(copies)]
    for move in moves:
        move.start()
    return moves


def copy_all(copies, done):
    for move in start_all(copies, done):
        move.wait()


def split_times_kernel(place_ref, chi_ref, *refs):
    targets = [place_ref[1] ^ step for step in range(4)]
    copies = [(chi_ref.at[t, target % 2, target // 2], refs[step].at[t]) for step, target in enumerate(targets) for t in range(4)]
    copy_all(copies, refs[4])


def split_rows_kernel(place_ref, green_ref, *refs):
    held, read, written = refs[4:]
    starts = [jnp.minimum(4 * (place_ref[0] ^ step), GROUPS - 4) for step in range(4)]
    moves = start_all([(green_ref.at[:, pl.ds(start, 4)], held.at[step]) for step, start in enumerate(starts)], read)
    for step, move in enumerate(moves):
        move.wait()
        pltpu.make_async_copy(held.at[step], refs[step], written.at[step]).start()
    for step in range(4):
        pltpu.make_async_copy(held.at[step], refs[step], written.at[step]).wait()


def split_groups_kernel(place_ref, *refs):
    held, read, written = refs[8:]
    copy_all([(refs[part].at[:, place_ref[1] ^ step], held.at[step, part]) for step in range(4) for part in range(4)], read)
    copy_all([(held.at[step], refs[4 + step]) for step in range(4)], written)


def arrived_kernel(*refs):
    refs[-1][...] = jnp.zeros((8, 128), jnp.float32)


ANY = pl.BlockSpec(memory_space=pl.ANY)
SMEM = pl.BlockSpec(memory_space=pltpu.SMEM)
VMEM = pl.BlockSpec(memory_space=pltpu.VMEM)
HBM = pl.BlockSpec(memory_space=pltpu.HBM)


def in_hbm(array):
    return pltpu.with_memory_space_constraint(array, pltpu.HBM)


def in_vmem(array):
    return pltpu.with_memory_space_constraint(array, pltpu.VMEM)


def copies_call(kernel, outs, space, inputs, scratch, cost=None):
    return pl.pallas_call(
        kernel,
        out_shape=outs,
        in_specs=[SMEM] + [ANY] * inputs,
        out_specs=[space] * len(outs),
        scratch_shapes=scratch,
        compiler_params=pltpu.CompilerParams(vmem_limit_bytes=4 * MIB),
        cost_estimate=cost,
    )


def sems(count):
    return pltpu.SemaphoreType.DMA((count,))


def local(chi_time, green, band_coeffs):
    mom = lax.axis_index("mom")
    tm = lax.axis_index("zlo") * 2 + lax.axis_index("core")
    place = jnp.stack([mom, tm]).astype(jnp.int32)
    wide, narrow, back = [lax.dynamic_index_in_dim(jnp.asarray(tables), tm, 0, False) for tables in mixing_tables()]
    vmem = lambda mib: pltpu.CompilerParams(vmem_limit_bytes=mib * MIB)
    long = pl.CostEstimate(flops=100000000000, transcendentals=0, bytes_accessed=4 * MIB)

    pieces = copies_call(split_times_kernel, [pltpu.VMEM((4, 56, NP), jnp.bfloat16)] * 4, VMEM, 1, [sems(16)])(place, in_hbm(chi_time.reshape(4, 2, 2, 56, NP)))
    received = [pieces[0]] + [swap(pieces[step], TM, step) for step in (1, 2, 3)]

    parts = copies_call(
        split_rows_kernel,
        [pltpu.HBM((8, 4, 8, NP), jnp.bfloat16)] * 4,
        HBM,
        1,
        [pltpu.VMEM((4, 8, 4, 8, NP), jnp.bfloat16), sems(4), sems(4)],
        cost=long,
    )(place, in_hbm(green.reshape(8, GROUPS, 8, NP)))
    by_mom = [parts[0]] + [swap(parts[step], "mom", step) for step in (1, 2, 3)]

    mixed = pl.pallas_call(
        frequency_kernel,
        out_shape=pltpu.HBM((NT, 56, NP), jnp.bfloat16),
        out_specs=HBM,
        scratch_shapes=[pltpu.VMEM((NT, 56, NP), jnp.bfloat16), sems(4)],
        compiler_params=vmem(8),
        cost_estimate=long,
    )(*received, wide, narrow)
    groups = copies_call(
        split_groups_kernel,
        [pltpu.HBM((4, 8, 8, NP), jnp.bfloat16)] * 4,
        HBM,
        4,
        [pltpu.VMEM((4, 4, 8, 8, NP), jnp.bfloat16), sems(16), sems(4)],
        cost=long,
    )(place, *by_mom)
    tile = exchange(mixed, PLANE).reshape(NP, NP)
    tile, groups = lax.optimization_barrier((tile, groups))
    cells = [groups[0]] + [swap(groups[step], TM, step) for step in (1, 2, 3)]
    cells = [cell.reshape(4, 64, NP) for cell in cells]
    arrived = pl.pallas_call(
        arrived_kernel, out_shape=jax.ShapeDtypeStruct((8, 128), jnp.float32), in_specs=[ANY] * 4, cost_estimate=long
    )(*cells)

    square = pltpu.VMEM((NP, NP), jnp.bfloat16)
    screened = pl.pallas_call(
        series_kernel,
        out_shape=pltpu.HBM((1024, NP), jnp.bfloat16),
        out_specs=HBM,
        scratch_shapes=[square, square, pltpu.VMEM((NP, NP), jnp.float32), square, square]
        + [pltpu.VMEM((1024, NP), jnp.bfloat16), pltpu.SemaphoreType.DMA((4,))],
        compiler_params=vmem(16),
        cost_estimate=long,
    )(tile)
    spread = exchange(screened.reshape(128, 8, NP), BY_ROWS).reshape(1024, NP)

    group = jnp.minimum(4 * mom, GROUPS - 4) + tm
    row = (lax.axis_index("x") * 2 + lax.axis_index("zhi")) * 112 + 8 * group
    own = lax.dynamic_slice_in_dim(band_coeffs, row, 8, 0)
    partial_sums = pl.pallas_call(
        self_energy_kernel,
        out_shape=jax.ShapeDtypeStruct((16, 8, 8, 128), jnp.bfloat16),
        in_specs=[SMEM] + [VMEM] * 8,
        scratch_shapes=[pltpu.VMEM((4, 256, NP), jnp.float32), pltpu.VMEM((4, 256, NP), jnp.bfloat16)],
        compiler_params=vmem(12),
    )(place, in_vmem(spread), back, *cells, jnp.concatenate([band_coeffs, own], axis=0), arrived)
    shares = exchange(partial_sums.reshape(128, 8, 128), BY_OUTPUT)
    return shares.astype(jnp.float32).sum(axis=0).reshape(2, 4, 128)


def solution(mesh):
    fine = Mesh(mesh.devices.reshape(4, 2, 2, 4, 2), ("mom", "zlo", "core", "x", "zhi"))
    placed = (P(TM, "mom", ("x", "zhi"), None), P("mom", TM, ("x", "zhi"), None), P())
    return jax.shard_map(
        local, mesh=fine, in_specs=placed, out_specs=P("mom", TM, ("x", "zhi")), check_vma=False
    )
```

```python
import math

import jax
import jax.numpy as jnp
import ml_dtypes
import numpy as np
from jax import lax
from jax.experimental import pallas as pl
from jax.experimental.pallas import tpu as pltpu
from jax.sharding import Mesh
from jax.sharding import PartitionSpec as P

COUPLING = 0.8
NT, NK, NP, NB = 16, 8, 896, 1024
GROUPS = 14

C5 = (math.sqrt(22.0) - 1.0) / 4.0
C3 = 0.75 - C5
C4 = 0.625
C6 = 2.0 - 1.25 * C5

TM = ("zlo", "core")
PLANE = ("x", "zhi", "zlo")
BY_ROWS = ("x", "zhi", "mom", "zlo", "core")
BY_OUTPUT = ("mom", "zlo", "core", "x", "zhi")
MIB = 1024 * 1024


def exchange(pieces, axes):
    return lax.all_to_all(pieces, axes, split_axis=0, concat_axis=0, tiled=True)


def swap(piece, axes, step):
    return lax.ppermute(piece, axes, [(i, i ^ step) for i in range(4)])


def mixing_tables():
    index = np.arange(NT) + 0.5
    cosine = (np.sqrt(2.0 / NT) * np.cos(np.pi * index[:, None] * index[None, :] / NT)).astype(np.float32)
    wide, narrow, back = [], [], []
    for tm in range(4):
        times = [4 * ((place // 4) ^ tm) + place % 4 for place in range(NT)]
        wide.append(np.kron(cosine[:, times], np.eye(16)))
        narrow.append(np.kron(cosine[:, times], np.eye(8)))
        back.append(np.einsum("tw,cd,ab->ctawdb", cosine[times, :], np.eye(2), np.eye(8)).reshape(256, 256))
    return [np.stack(tables).astype(ml_dtypes.bfloat16) for tables in (wide, narrow, back)]


def frequency_kernel(own_ref, first_ref, second_ref, third_ref, wide_ref, narrow_ref, out_ref, mixed_ref, sent):
    pieces = (own_ref, first_ref, second_ref, third_ref)
    scale = COUPLING / math.sqrt(NP)
    rows = jnp.concatenate([piece[t, 48:56, :].astype(jnp.float32) for piece in pieces for t in range(4)], axis=0)
    mixed = jnp.dot(narrow_ref[...], rows.astype(jnp.bfloat16), preferred_element_type=jnp.float32) * scale
    mixed_ref[:, 48:56, :] = mixed.reshape(NT, 8, NP).astype(jnp.bfloat16)
    for at in range(0, 48, 16):
        rows = jnp.concatenate([piece[t, at : at + 16, :] for piece in pieces for t in range(4)], axis=0)
        mixed = jnp.dot(wide_ref[...], rows, preferred_element_type=jnp.float32) * scale
        mixed_ref[:, at : at + 16, :] = mixed.reshape(NT, 16, NP).astype(jnp.bfloat16)
    copy_all([(mixed_ref.at[pl.ds(4 * i, 4)], out_ref.at[pl.ds(4 * i, 4)]) for i in range(4)], sent)


def series_kernel(tile_ref, out_ref, square_ref, sum_ref, fourth_ref, left_ref, right_ref, padded_ref, sent):
    step = 224
    for at in range(0, NP, step):
        rows = slice(at, at + step)
        square = jnp.dot(tile_ref[rows, :], tile_ref[...], preferred_element_type=jnp.float32).astype(jnp.bfloat16)
        square_ref[rows, :] = square
        sum_ref[rows, :] = (square.astype(jnp.float32) + 0.5 * tile_ref[rows, :].astype(jnp.float32)).astype(jnp.bfloat16)
    for at in range(0, NP, step):
        rows = slice(at, at + step)
        fourth = jnp.dot(square_ref[rows, :], sum_ref[...], preferred_element_type=jnp.float32)
        square = square_ref[rows, :].astype(jnp.float32)
        tile = tile_ref[rows, :].astype(jnp.float32)
        left_ref[rows, :] = (fourth + C3 * square + C4 * tile).astype(jnp.bfloat16)
        right_ref[rows, :] = (fourth + C5 * square).astype(jnp.bfloat16)
        fourth_ref[rows, :] = C6 * fourth + square + tile
    sends = []
    for at, count in (0, 224), (224, 224), (448, 224), (672, 112), (784, 112):
        rows = slice(at, at + count)
        total = jnp.dot(left_ref[rows, :], right_ref[...], preferred_element_type=jnp.float32) + fourth_ref[rows, :]
        total = total.astype(jnp.bfloat16)
        for half in range(count // 112):
            to = 128 * (at // 112 + half)
            padded_ref[to : to + 96, :] = total[112 * half : 112 * half + 96]
            padded_ref[to + 96 : to + 112, :] = jnp.zeros((16, NP), jnp.bfloat16)
            padded_ref[to + 112 : to + 128, :] = total[112 * half + 96 : 112 * half + 112]
        rows = pl.ds(128 * (at // 112), 128 * (count // 112))
        sends.append(pltpu.make_async_copy(padded_ref.at[rows], out_ref.at[rows], sent.at[len(sends)]))
        sends[-1].start()
    for send in sends:
        send.wait()


def hartley8(x):
    root = math.sqrt(2.0)
    a0, a1, a2, a3 = x[0] + x[4], x[1] + x[5], x[2] + x[6], x[3] + x[7]
    b0, b1, b2, b3 = x[0] - x[4], x[1] - x[5], x[2] - x[6], x[3] - x[7]
    c0, c1, d0, d1 = a0 + a2, a1 + a3, a0 - a2, a1 - a3
    e0, e1, f1, f3 = b0 + b2, b0 - b2, root * b1, root * b3
    return [c0 + c1, e0 + f1, d0 + d1, e1 + f3, c0 - c1, e0 - f1, d0 - d1, e1 - f3]


def self_energy_kernel(place_ref, screened_ref, table_ref, *refs):
    cell_refs, (coeffs_hbm, own_ref, _, out_ref, time_ref, sigma_ref, coeffs_ref, held_ref, fetched) = list(refs[:4]), refs[4:]
    parts = [pl.ds(448 * i, 448) for i in range(2)]
    moves = start_all([(coeffs_hbm.at[part], coeffs_ref.at[part]) for part in parts] + [(cell_refs[0], held_ref)], fetched)
    cell_refs[0] = held_ref
    mom_here, tm_here = place_ref[0], place_ref[1]
    table = table_ref[...]
    for mom in range(4):
        rows = jnp.concatenate([screened_ref[128 * p + 32 * mom : 128 * p + 32 * mom + 32, :] for p in range(8)], axis=0)
        time_ref[mom] = jnp.dot(table, rows, preferred_element_type=jnp.float32)
    norm = 1.0 / math.sqrt(NK)
    own = own_ref[...].astype(jnp.float32)
    for step in (1, 2, 3, 0):
        if step == 0:
            moves[2].wait()
        for pair in range(2):
            at = 32 * step + 16 * pair
            tiles = [time_ref[k // 2, 128 * (k % 2) + at : 128 * (k % 2) + at + 16, :] * norm for k in range(NK)]
            cells = hartley8(tiles)
            for r in range(NK):
                at = 32 * (r % 2) + 16 * pair
                value = cell_refs[step][(r // 2) ^ mom_here, at : at + 16, :].astype(jnp.float32) * cells[r]
                sigma_ref[step, 64 * (r // 2) + at : 64 * (r // 2) + at + 16, :] = value.astype(jnp.bfloat16)
        if step == 1:
            for move in moves[:2]:
                move.wait()
        applied = jnp.dot(sigma_ref[step], coeffs_ref[...], preferred_element_type=jnp.float32)
        values = jnp.sum(applied.reshape(32, 8, NB) * own[None], axis=1)
        for mom in range(4):
            for p in range(8):
                share = values[8 * mom : 8 * mom + 8, 128 * p : 128 * p + 128]
                out_ref[4 * mom + (tm_here ^ step), p] = share.astype(out_ref.dtype)


def start_all(copies, done):
    moves = [pltpu.make_async_copy(source, target, done.at[i]) for i, (source, target) in enumerate(copies)]
    for move in moves:
        move.start()
    return moves


def copy_all(copies, done):
    for move in start_all(copies, done):
        move.wait()


def split_times_kernel(place_ref, chi_ref, *refs):
    held, read, written = refs[4:]
    order = (3, 2, 1, 0)
    targets = [place_ref[1] ^ step for step in order]
    into = [refs[0] if step == 0 else held.at[step - 1] for step in order]
    reads = start_all([(chi_ref.at[:, target % 2, target // 2], to) for target, to in zip(targets, into)], read)
    writes = []
    for step, move in zip(order, reads):
        move.wait()
        if step:
            writes += start_all([(held.at[step - 1], refs[step])], written.at[pl.ds(step, 1)])
    for move in writes:
        move.wait()


def split_rows_kernel(place_ref, green_ref, *refs):
    held, read, written = refs[4:]
    starts = [jnp.minimum(4 * (place_ref[0] ^ step), GROUPS - 4) for step in range(4)]
    moves = start_all([(green_ref.at[:, pl.ds(start, 4)], held.at[step]) for step, start in enumerate(starts)], read)
    for step, move in enumerate(moves):
        move.wait()
        pltpu.make_async_copy(held.at[step], refs[step], written.at[step]).start()
    for step in range(4):
        pltpu.make_async_copy(held.at[step], refs[step], written.at[step]).wait()


def split_groups_kernel(place_ref, *refs):
    held, read, written = refs[8:]
    copy_all([(refs[part].at[:, place_ref[1] ^ step], held.at[step, part]) for step in range(4) for part in range(4)], read)
    copy_all([(held.at[step], refs[4 + step]) for step in range(4)], written)


def arrived_kernel(*refs):
    refs[-1][...] = jnp.zeros((8, 128), jnp.float32)


ANY = pl.BlockSpec(memory_space=pl.ANY)
SMEM = pl.BlockSpec(memory_space=pltpu.SMEM)
VMEM = pl.BlockSpec(memory_space=pltpu.VMEM)
HBM = pl.BlockSpec(memory_space=pltpu.HBM)


def in_hbm(array):
    return pltpu.with_memory_space_constraint(array, pltpu.HBM)


def in_vmem(array):
    return pltpu.with_memory_space_constraint(array, pltpu.VMEM)


def copies_call(kernel, outs, space, inputs, scratch, cost=None):
    return pl.pallas_call(
        kernel,
        out_shape=outs,
        in_specs=[SMEM] + [ANY] * inputs,
        out_specs=[space] * len(outs),
        scratch_shapes=scratch,
        compiler_params=pltpu.CompilerParams(vmem_limit_bytes=4 * MIB),
        cost_estimate=cost,
    )


def sems(count):
    return pltpu.SemaphoreType.DMA((count,))


def local(chi_time, green, band_coeffs):
    mom = lax.axis_index("mom")
    tm = lax.axis_index("zlo") * 2 + lax.axis_index("core")
    place = jnp.stack([mom, tm]).astype(jnp.int32)
    wide, narrow, back = [lax.dynamic_index_in_dim(jnp.asarray(tables), tm, 0, False) for tables in mixing_tables()]
    vmem = lambda mib: pltpu.CompilerParams(vmem_limit_bytes=mib * MIB)
    long = pl.CostEstimate(flops=100000000000, transcendentals=0, bytes_accessed=4 * MIB)

    quarter = (4, 56, NP)
    pieces = pl.pallas_call(
        split_times_kernel,
        out_shape=[jax.ShapeDtypeStruct(quarter, jnp.bfloat16)] + [pltpu.HBM(quarter, jnp.bfloat16)] * 3,
        in_specs=[SMEM, HBM],
        out_specs=[VMEM] + [HBM] * 3,
        scratch_shapes=[pltpu.VMEM((3, *quarter), jnp.bfloat16), sems(4), sems(4)],
        compiler_params=vmem(4),
    )(place, in_hbm(chi_time.reshape(4, 2, 2, 56, NP)))
    received = [pieces[0]] + [swap(pieces[step], TM, step) for step in (1, 2, 3)]

    parts = copies_call(
        split_rows_kernel,
        [pltpu.HBM((8, 4, 8, NP), jnp.bfloat16)] * 4,
        HBM,
        1,
        [pltpu.VMEM((4, 8, 4, 8, NP), jnp.bfloat16), sems(4), sems(4)],
        cost=long,
    )(place, in_hbm(green.reshape(8, GROUPS, 8, NP)))
    by_mom = [parts[0]] + [swap(parts[step], "mom", step) for step in (1, 2, 3)]

    mixed = pl.pallas_call(
        frequency_kernel,
        out_shape=pltpu.HBM((NT, 56, NP), jnp.bfloat16),
        out_specs=HBM,
        scratch_shapes=[pltpu.VMEM((NT, 56, NP), jnp.bfloat16), sems(4)],
        compiler_params=vmem(8),
        cost_estimate=long,
    )(*received, wide, narrow)
    groups = copies_call(
        split_groups_kernel,
        [pltpu.HBM((4, 8, 8, NP), jnp.bfloat16)] * 4,
        HBM,
        4,
        [pltpu.VMEM((4, 4, 8, 8, NP), jnp.bfloat16), sems(16), sems(4)],
        cost=long,
    )(place, *by_mom)
    tile = exchange(mixed, PLANE).reshape(NP, NP)
    tile, groups = lax.optimization_barrier((tile, groups))
    cells = [groups[0]] + [swap(groups[step], TM, step) for step in (1, 2, 3)]
    cells = [cell.reshape(4, 64, NP) for cell in cells]
    arrived = pl.pallas_call(
        arrived_kernel,
        out_shape=jax.ShapeDtypeStruct((8, 128), jnp.float32),
        in_specs=[VMEM] * 2,
        compiler_params=vmem(1),
        cost_estimate=long,
    )(*cells[2:])

    square = pltpu.VMEM((NP, NP), jnp.bfloat16)
    screened = pl.pallas_call(
        series_kernel,
        out_shape=pltpu.HBM((1024, NP), jnp.bfloat16),
        out_specs=HBM,
        scratch_shapes=[square, square, pltpu.VMEM((NP, NP), jnp.float32), square, square]
        + [pltpu.VMEM((1024, NP), jnp.bfloat16), sems(5)],
        compiler_params=vmem(16),
        cost_estimate=long,
    )(tile)
    spread = exchange(screened.reshape(128, 8, NP), BY_ROWS).reshape(1024, NP)

    group = jnp.minimum(4 * mom, GROUPS - 4) + tm
    row = (lax.axis_index("x") * 2 + lax.axis_index("zhi")) * 112 + 8 * group
    own = lax.dynamic_slice_in_dim(band_coeffs, row, 8, 0)
    partial_sums = pl.pallas_call(
        self_energy_kernel,
        out_shape=jax.ShapeDtypeStruct((16, 8, 8, 128), jnp.bfloat16),
        in_specs=[SMEM, VMEM, VMEM, HBM, VMEM, VMEM, VMEM, HBM, VMEM, HBM],
        scratch_shapes=[pltpu.VMEM((4, 256, NP), jnp.float32), pltpu.VMEM((4, 256, NP), jnp.bfloat16)]
        + [pltpu.VMEM((NP, NB), jnp.bfloat16), pltpu.VMEM((4, 64, NP), jnp.bfloat16), sems(3)],
        compiler_params=vmem(12),
    )(place, in_vmem(spread), back, in_hbm(cells[0]), *cells[1:], in_hbm(band_coeffs), own, in_hbm(arrived))
    shares = exchange(partial_sums.reshape(128, 8, 128), BY_OUTPUT)
    return shares.astype(jnp.float32).sum(axis=0).reshape(2, 4, 128)


def solution(mesh):
    fine = Mesh(mesh.devices.reshape(4, 2, 2, 4, 2), ("mom", "zlo", "core", "x", "zhi"))
    placed = (P(TM, "mom", ("x", "zhi"), None), P("mom", TM, ("x", "zhi"), None), P())
    return jax.shard_map(
        local, mesh=fine, in_specs=placed, out_specs=P("mom", TM, ("x", "zhi")), check_vma=False
    )
```

```python
import math

import jax
import jax.numpy as jnp
import ml_dtypes
import numpy as np
from jax import lax
from jax.experimental import pallas as pl
from jax.experimental.pallas import tpu as pltpu
from jax.sharding import Mesh
from jax.sharding import PartitionSpec as P

COUPLING = 0.8
NT, NK, NP, NB = 16, 8, 896, 1024
GROUPS = 14

C5 = (math.sqrt(22.0) - 1.0) / 4.0
C3 = 0.75 - C5
C4 = 0.625
C6 = 2.0 - 1.25 * C5

TM = ("zlo", "core")
PLANE = ("x", "zhi", "zlo")
BY_ROWS = ("x", "zhi", "mom", "zlo", "core")
BY_OUTPUT = ("mom", "zlo", "core", "x", "zhi")
MIB = 1024 * 1024


def exchange(pieces, axes):
    return lax.all_to_all(pieces, axes, split_axis=0, concat_axis=0, tiled=True)


def swap(piece, axes, step):
    return lax.ppermute(piece, axes, [(i, i ^ step) for i in range(4)])


def mixing_tables():
    index = np.arange(NT) + 0.5
    cosine = (np.sqrt(2.0 / NT) * np.cos(np.pi * index[:, None] * index[None, :] / NT)).astype(np.float32)
    wide, narrow, back = [], [], []
    for tm in range(4):
        times = [4 * ((place // 4) ^ tm) + place % 4 for place in range(NT)]
        wide.append(np.kron(cosine[:, times], np.eye(16)))
        narrow.append(np.kron(cosine[:, times], np.eye(8)))
        back.append(np.einsum("tw,cd,ab->ctawdb", cosine[times, :], np.eye(2), np.eye(8)).reshape(256, 256))
    return [np.stack(tables).astype(ml_dtypes.bfloat16) for tables in (wide, narrow, back)]


def frequency_kernel(own_ref, first_ref, second_ref, third_ref, wide_ref, narrow_ref, out_ref, mixed_ref, sent):
    pieces = (own_ref, first_ref, second_ref, third_ref)
    scale = COUPLING / math.sqrt(NP)
    rows = jnp.concatenate([piece[t, 48:56, :].astype(jnp.float32) for piece in pieces for t in range(4)], axis=0)
    mixed = jnp.dot(narrow_ref[...], rows.astype(jnp.bfloat16), preferred_element_type=jnp.float32) * scale
    mixed_ref[:, 48:56, :] = mixed.reshape(NT, 8, NP).astype(jnp.bfloat16)
    moves = start_all([(mixed_ref.at[:, pl.ds(48, 8)], out_ref.at[:, pl.ds(48, 8)])], sent.at[pl.ds(0, 1)])
    for at in range(0, 48, 16):
        rows = jnp.concatenate([piece[t, at : at + 16, :] for piece in pieces for t in range(4)], axis=0)
        mixed = jnp.dot(wide_ref[...], rows, preferred_element_type=jnp.float32) * scale
        mixed_ref[:, at : at + 16, :] = mixed.reshape(NT, 16, NP).astype(jnp.bfloat16)
        moves += start_all([(mixed_ref.at[:, pl.ds(at, 16)], out_ref.at[:, pl.ds(at, 16)])], sent.at[pl.ds(1 + at // 16, 1)])
    for move in moves:
        move.wait()


def series_kernel(tile_ref, out_ref, square_ref, sum_ref, fourth_ref, left_ref, right_ref, padded_ref, sent):
    step = 224
    for at in range(0, NP, step):
        rows = slice(at, at + step)
        square = jnp.dot(tile_ref[rows, :], tile_ref[...], preferred_element_type=jnp.float32).astype(jnp.bfloat16)
        square_ref[rows, :] = square
        sum_ref[rows, :] = (square.astype(jnp.float32) + 0.5 * tile_ref[rows, :].astype(jnp.float32)).astype(jnp.bfloat16)
    for at in range(0, NP, step):
        rows = slice(at, at + step)
        fourth = jnp.dot(square_ref[rows, :], sum_ref[...], preferred_element_type=jnp.float32)
        square = square_ref[rows, :].astype(jnp.float32)
        tile = tile_ref[rows, :].astype(jnp.float32)
        left_ref[rows, :] = (fourth + C3 * square + C4 * tile).astype(jnp.bfloat16)
        right_ref[rows, :] = (fourth + C5 * square).astype(jnp.bfloat16)
        fourth_ref[rows, :] = C6 * fourth + square + tile
    sends = []
    for at, count in (0, 224), (224, 224), (448, 224), (672, 112), (784, 112):
        rows = slice(at, at + count)
        total = jnp.dot(left_ref[rows, :], right_ref[...], preferred_element_type=jnp.float32) + fourth_ref[rows, :]
        total = total.astype(jnp.bfloat16)
        for half in range(count // 112):
            to = 128 * (at // 112 + half)
            padded_ref[to : to + 96, :] = total[112 * half : 112 * half + 96]
            padded_ref[to + 96 : to + 112, :] = jnp.zeros((16, NP), jnp.bfloat16)
            padded_ref[to + 112 : to + 128, :] = total[112 * half + 96 : 112 * half + 112]
        rows = pl.ds(128 * (at // 112), 128 * (count // 112))
        sends.append(pltpu.make_async_copy(padded_ref.at[rows], out_ref.at[rows], sent.at[len(sends)]))
        sends[-1].start()
    for send in sends:
        send.wait()


def hartley8(x):
    root = math.sqrt(2.0)
    a0, a1, a2, a3 = x[0] + x[4], x[1] + x[5], x[2] + x[6], x[3] + x[7]
    b0, b1, b2, b3 = x[0] - x[4], x[1] - x[5], x[2] - x[6], x[3] - x[7]
    c0, c1, d0, d1 = a0 + a2, a1 + a3, a0 - a2, a1 - a3
    e0, e1, f1, f3 = b0 + b2, b0 - b2, root * b1, root * b3
    return [c0 + c1, e0 + f1, d0 + d1, e1 + f3, c0 - c1, e0 - f1, d0 - d1, e1 - f3]


def self_energy_kernel(place_ref, screened_ref, table_ref, *refs):
    cell_refs, (coeffs_hbm, own_ref, _, out_ref, time_ref, sigma_ref, coeffs_ref, held_ref, fetched) = list(refs[:4]), refs[4:]
    parts = [pl.ds(448 * i, 448) for i in range(2)]
    moves = start_all([(coeffs_hbm.at[part], coeffs_ref.at[part]) for part in parts] + [(cell_refs[0], held_ref)], fetched)
    cell_refs[0] = held_ref
    mom_here, tm_here = place_ref[0], place_ref[1]
    table = table_ref[...]
    for mom in range(4):
        rows = jnp.concatenate([screened_ref[128 * p + 32 * mom : 128 * p + 32 * mom + 32, :] for p in range(8)], axis=0)
        time_ref[mom] = jnp.dot(table, rows, preferred_element_type=jnp.float32)
    norm = 1.0 / math.sqrt(NK)
    own = own_ref[...].astype(jnp.float32)
    for step in (1, 2, 3, 0):
        if step == 0:
            moves[2].wait()
        for pair in range(2):
            at = 32 * step + 16 * pair
            tiles = [time_ref[k // 2, 128 * (k % 2) + at : 128 * (k % 2) + at + 16, :] * norm for k in range(NK)]
            cells = hartley8(tiles)
            for r in range(NK):
                at = 32 * (r % 2) + 16 * pair
                value = cell_refs[step][(r // 2) ^ mom_here, at : at + 16, :].astype(jnp.float32) * cells[r]
                sigma_ref[step, 64 * (r // 2) + at : 64 * (r // 2) + at + 16, :] = value.astype(jnp.bfloat16)
        if step == 1:
            for move in moves[:2]:
                move.wait()
        applied = jnp.dot(sigma_ref[step], coeffs_ref[...], preferred_element_type=jnp.float32)
        values = row_sums(applied.reshape(32, 8, NB) * own[None])
        for mom in range(4):
            for p in range(8):
                share = values[8 * mom : 8 * mom + 8, 128 * p : 128 * p + 128]
                out_ref[4 * mom + (tm_here ^ step), p] = share.astype(out_ref.dtype)


def row_sums(x):
    n = x.shape[-1]
    x = x.reshape(4, 8, 8, n)
    row = lax.broadcasted_iota(jnp.int32, (1, 1, 8, n), 2)
    turn = lambda v, by: pltpu.roll(v.reshape(-1, 8, n), by, 1).reshape(v.shape)
    for half in (4, 2, 1):
        low, high = x[:, :half], x[:, half:]
        x = jnp.where(row % (2 * half) < half, low + turn(low, 8 - half), high + turn(high, half))
    return x.reshape(32, n)


def start_all(copies, done):
    moves = [pltpu.make_async_copy(source, target, done.at[i]) for i, (source, target) in enumerate(copies)]
    for move in moves:
        move.start()
    return moves


def copy_all(copies, done):
    for move in start_all(copies, done):
        move.wait()


def split_times_kernel(place_ref, chi_ref, *refs):
    held, read, written = refs[4:]
    order = (3, 2, 1, 0)
    targets = [place_ref[1] ^ step for step in order]
    into = [refs[0] if step == 0 else held.at[step - 1] for step in order]
    reads = start_all([(chi_ref.at[:, target % 2, target // 2], to) for target, to in zip(targets, into)], read)
    writes = []
    for step, move in zip(order, reads):
        move.wait()
        if step:
            writes += start_all([(held.at[step - 1], refs[step])], written.at[pl.ds(step, 1)])
    for move in writes:
        move.wait()


def split_rows_kernel(place_ref, green_ref, *refs):
    held, read, written = refs[4:]
    starts = [jnp.minimum(4 * (place_ref[0] ^ step), GROUPS - 4) for step in range(4)]
    moves = start_all([(green_ref.at[:, pl.ds(start, 4)], held.at[step]) for step, start in enumerate(starts)], read)
    for step, move in enumerate(moves):
        move.wait()
        pltpu.make_async_copy(held.at[step], refs[step], written.at[step]).start()
    for step in range(4):
        pltpu.make_async_copy(held.at[step], refs[step], written.at[step]).wait()


def split_groups_kernel(place_ref, *refs):
    held, read, written = refs[8:]
    copy_all([(refs[part].at[:, place_ref[1] ^ step], held.at[step, part]) for step in range(4) for part in range(4)], read)
    copy_all([(held.at[step], refs[4 + step]) for step in range(4)], written)


def arrived_kernel(*refs):
    refs[-1][...] = jnp.zeros((8, 128), jnp.float32)


ANY = pl.BlockSpec(memory_space=pl.ANY)
SMEM = pl.BlockSpec(memory_space=pltpu.SMEM)
VMEM = pl.BlockSpec(memory_space=pltpu.VMEM)
HBM = pl.BlockSpec(memory_space=pltpu.HBM)


def in_hbm(array):
    return pltpu.with_memory_space_constraint(array, pltpu.HBM)


def in_vmem(array):
    return pltpu.with_memory_space_constraint(array, pltpu.VMEM)


def copies_call(kernel, outs, space, inputs, scratch, cost=None):
    return pl.pallas_call(
        kernel,
        out_shape=outs,
        in_specs=[SMEM] + [ANY] * inputs,
        out_specs=[space] * len(outs),
        scratch_shapes=scratch,
        compiler_params=pltpu.CompilerParams(vmem_limit_bytes=4 * MIB),
        cost_estimate=cost,
    )


def sems(count):
    return pltpu.SemaphoreType.DMA((count,))


def local(chi_time, green, band_coeffs):
    mom = lax.axis_index("mom")
    tm = lax.axis_index("zlo") * 2 + lax.axis_index("core")
    place = jnp.stack([mom, tm]).astype(jnp.int32)
    wide, narrow, back = [lax.dynamic_index_in_dim(jnp.asarray(tables), tm, 0, False) for tables in mixing_tables()]
    vmem = lambda mib: pltpu.CompilerParams(vmem_limit_bytes=mib * MIB)
    long = pl.CostEstimate(flops=100000000000, transcendentals=0, bytes_accessed=4 * MIB)

    quarter = (4, 56, NP)
    pieces = pl.pallas_call(
        split_times_kernel,
        out_shape=[jax.ShapeDtypeStruct(quarter, jnp.bfloat16)] + [pltpu.HBM(quarter, jnp.bfloat16)] * 3,
        in_specs=[SMEM, HBM],
        out_specs=[VMEM] + [HBM] * 3,
        scratch_shapes=[pltpu.VMEM((3, *quarter), jnp.bfloat16), sems(4), sems(4)],
        compiler_params=vmem(4),
    )(place, in_hbm(chi_time.reshape(4, 2, 2, 56, NP)))
    pieces = list(pieces)

    green, pieces[1] = lax.optimization_barrier((green, pieces[1]))
    parts = copies_call(
        split_rows_kernel,
        [pltpu.HBM((8, 4, 8, NP), jnp.bfloat16)] * 4,
        HBM,
        1,
        [pltpu.VMEM((4, 8, 4, 8, NP), jnp.bfloat16), sems(4), sems(4)],
        cost=long,
    )(place, in_hbm(green.reshape(8, GROUPS, 8, NP)))
    received = [pieces[0]] + [swap(pieces[step], TM, step) for step in (1, 2, 3)]
    by_mom = [parts[0]] + [swap(parts[step], "mom", step) for step in (1, 2, 3)]

    mixed = pl.pallas_call(
        frequency_kernel,
        out_shape=pltpu.HBM((NT, 56, NP), jnp.bfloat16),
        out_specs=HBM,
        scratch_shapes=[pltpu.VMEM((NT, 56, NP), jnp.bfloat16), sems(4)],
        compiler_params=vmem(8),
        cost_estimate=long,
    )(*received, wide, narrow)
    groups = copies_call(
        split_groups_kernel,
        [pltpu.HBM((4, 8, 8, NP), jnp.bfloat16)] * 4,
        HBM,
        4,
        [pltpu.VMEM((4, 4, 8, 8, NP), jnp.bfloat16), sems(16), sems(4)],
        cost=long,
    )(place, *by_mom)
    tile = exchange(mixed, PLANE).reshape(NP, NP)
    cells = [groups[0]] + [swap(groups[step], TM, step) for step in (1, 2, 3)]
    cells = [cell.reshape(4, 64, NP) for cell in cells]
    arrived = pl.pallas_call(
        arrived_kernel,
        out_shape=jax.ShapeDtypeStruct((8, 128), jnp.float32),
        in_specs=[VMEM] * 2,
        compiler_params=vmem(1),
        cost_estimate=long,
    )(*cells[2:])

    square = pltpu.VMEM((NP, NP), jnp.bfloat16)
    screened = pl.pallas_call(
        series_kernel,
        out_shape=pltpu.HBM((1024, NP), jnp.bfloat16),
        out_specs=HBM,
        scratch_shapes=[square, square, pltpu.VMEM((NP, NP), jnp.float32), square, square]
        + [pltpu.VMEM((1024, NP), jnp.bfloat16), sems(5)],
        compiler_params=vmem(16),
        cost_estimate=None,
    )(tile)
    spread = exchange(screened.reshape(128, 8, NP), BY_ROWS).reshape(1024, NP)

    group = jnp.minimum(4 * mom, GROUPS - 4) + tm
    row = (lax.axis_index("x") * 2 + lax.axis_index("zhi")) * 112 + 8 * group
    own = lax.dynamic_slice_in_dim(band_coeffs, row, 8, 0)
    partial_sums = pl.pallas_call(
        self_energy_kernel,
        out_shape=jax.ShapeDtypeStruct((16, 8, 8, 128), jnp.bfloat16),
        in_specs=[SMEM, VMEM, VMEM, HBM, VMEM, VMEM, VMEM, HBM, VMEM, HBM],
        scratch_shapes=[pltpu.VMEM((4, 256, NP), jnp.float32), pltpu.VMEM((4, 256, NP), jnp.bfloat16)]
        + [pltpu.VMEM((NP, NB), jnp.bfloat16), pltpu.VMEM((4, 64, NP), jnp.bfloat16), sems(3)],
        compiler_params=vmem(12),
    )(place, in_vmem(spread), back, in_hbm(cells[0]), *cells[1:], in_hbm(band_coeffs), own, in_hbm(arrived))
    shares = exchange(partial_sums.reshape(128, 8, 128), BY_OUTPUT)
    return shares.astype(jnp.float32).sum(axis=0).reshape(2, 4, 128)


def solution(mesh):
    fine = Mesh(mesh.devices.reshape(4, 2, 2, 4, 2), ("mom", "zlo", "core", "x", "zhi"))
    placed = (P(TM, "mom", ("x", "zhi"), None), P("mom", TM, ("x", "zhi"), None), P())
    return jax.shard_map(
        local, mesh=fine, in_specs=placed, out_specs=P("mom", TM, ("x", "zhi")), check_vma=False
    )
```

```python
import math

import jax
import jax.numpy as jnp
import ml_dtypes
import numpy as np
from jax import lax
from jax.experimental import pallas as pl
from jax.experimental.pallas import tpu as pltpu
from jax.sharding import Mesh
from jax.sharding import PartitionSpec as P

COUPLING = 0.8
NT, NK, NP, NB = 16, 8, 896, 1024
GROUPS = 14

C5 = (math.sqrt(22.0) - 1.0) / 4.0
C3 = 0.75 - C5
C4 = 0.625
C6 = 2.0 - 1.25 * C5

TM = ("zlo", "core")
PLANE = ("x", "zhi", "core")
BY_ROWS = ("x", "zhi", "mom", "zlo", "core")
BY_OUTPUT = ("mom", "zlo", "core", "x", "zhi")
MIB = 1024 * 1024


def exchange(pieces, axes):
    return lax.all_to_all(pieces, axes, split_axis=0, concat_axis=0, tiled=True)


def swap(piece, axes, step):
    return lax.ppermute(piece, axes, [(i, i ^ step) for i in range(4)])


def mixing_tables():
    index = np.arange(NT) + 0.5
    cosine = (np.sqrt(2.0 / NT) * np.cos(np.pi * index[:, None] * index[None, :] / NT)).astype(np.float32)
    wide, narrow, back = [], [], []
    for tm in range(4):
        times = [4 * ((place // 4) ^ tm) + place % 4 for place in range(NT)]
        wide.append(np.kron(cosine[:, times], np.eye(16)))
        narrow.append(np.kron(cosine[:, times], np.eye(8)))
        back.append(np.einsum("tpq,cd,ab->ctapdqb", cosine[times, :].reshape(NT, 8, 2), np.eye(2), np.eye(8)).reshape(256, 256))
    return [np.stack(tables).astype(ml_dtypes.bfloat16) for tables in (wide, narrow, back)]


def frequency_kernel(own_ref, first_ref, second_ref, third_ref, wide_ref, narrow_ref, out_ref, mixed_ref, sent):
    pieces = (own_ref, first_ref, second_ref, third_ref)
    scale = COUPLING / math.sqrt(NP)
    rows = jnp.concatenate([piece[t, 48:56, :].astype(jnp.float32) for piece in pieces for t in range(4)], axis=0)
    mixed = jnp.dot(narrow_ref[...], rows.astype(jnp.bfloat16), preferred_element_type=jnp.float32) * scale
    mixed_ref[:, 48:56, :] = mixed.reshape(NT, 8, NP).astype(jnp.bfloat16)
    moves = start_all([(mixed_ref.at[:, pl.ds(48, 8)], out_ref.at[:, pl.ds(48, 8)])], sent.at[pl.ds(0, 1)])
    for at in range(0, 48, 16):
        rows = jnp.concatenate([piece[t, at : at + 16, :] for piece in pieces for t in range(4)], axis=0)
        mixed = jnp.dot(wide_ref[...], rows, preferred_element_type=jnp.float32) * scale
        mixed_ref[:, at : at + 16, :] = mixed.reshape(NT, 16, NP).astype(jnp.bfloat16)
        moves += start_all([(mixed_ref.at[:, pl.ds(at, 16)], out_ref.at[:, pl.ds(at, 16)])], sent.at[pl.ds(1 + at // 16, 1)])
    for move in moves:
        move.wait()


def series_kernel(tile_ref, out_ref, square_ref, sum_ref, fourth_ref, left_ref, right_ref, padded_ref, sent):
    step = 224
    for at in range(0, NP, step):
        rows = slice(at, at + step)
        square = jnp.dot(tile_ref[rows, :], tile_ref[...], preferred_element_type=jnp.float32).astype(jnp.bfloat16)
        square_ref[rows, :] = square
        sum_ref[rows, :] = (square.astype(jnp.float32) + 0.5 * tile_ref[rows, :].astype(jnp.float32)).astype(jnp.bfloat16)
    for at in range(0, NP, step):
        rows = slice(at, at + step)
        fourth = jnp.dot(square_ref[rows, :], sum_ref[...], preferred_element_type=jnp.float32)
        square = square_ref[rows, :].astype(jnp.float32)
        tile = tile_ref[rows, :].astype(jnp.float32)
        left_ref[rows, :] = (fourth + C3 * square + C4 * tile).astype(jnp.bfloat16)
        right_ref[rows, :] = (fourth + C5 * square).astype(jnp.bfloat16)
        fourth_ref[rows, :] = C6 * fourth + square + tile
    sends = []
    for at, count in (0, 224), (224, 224), (448, 224), (672, 112), (784, 112):
        rows = slice(at, at + count)
        total = jnp.dot(left_ref[rows, :], right_ref[...], preferred_element_type=jnp.float32) + fourth_ref[rows, :]
        total = total.astype(jnp.bfloat16)
        for half in range(count // 112):
            to = 128 * (at // 112 + half)
            padded_ref[to : to + 96, :] = total[112 * half : 112 * half + 96]
            padded_ref[to + 96 : to + 112, :] = jnp.zeros((16, NP), jnp.bfloat16)
            padded_ref[to + 112 : to + 128, :] = total[112 * half + 96 : 112 * half + 112]
        rows = pl.ds(128 * (at // 112), 128 * (count // 112))
        sends.append(pltpu.make_async_copy(padded_ref.at[rows], out_ref.at[rows], sent.at[len(sends)]))
        sends[-1].start()
    for send in sends:
        send.wait()


def hartley8(x):
    root = math.sqrt(2.0)
    a0, a1, a2, a3 = x[0] + x[4], x[1] + x[5], x[2] + x[6], x[3] + x[7]
    b0, b1, b2, b3 = x[0] - x[4], x[1] - x[5], x[2] - x[6], x[3] - x[7]
    c0, c1, d0, d1 = a0 + a2, a1 + a3, a0 - a2, a1 - a3
    e0, e1, f1, f3 = b0 + b2, b0 - b2, root * b1, root * b3
    return [c0 + c1, e0 + f1, d0 + d1, e1 + f3, c0 - c1, e0 - f1, d0 - d1, e1 - f3]


def self_energy_kernel(place_ref, screened_ref, table_ref, *refs):
    cell_refs, (coeffs_hbm, own_ref, _, out_ref, time_ref, sigma_ref, coeffs_ref, held_ref, fetched) = list(refs[:4]), refs[4:]
    parts = [pl.ds(448 * i, 448) for i in range(2)]
    moves = start_all([(coeffs_hbm.at[part], coeffs_ref.at[part]) for part in parts] + [(cell_refs[0], held_ref)], fetched)
    cell_refs[0] = held_ref
    mom_here, tm_here = place_ref[0], place_ref[1]
    table = table_ref[...]
    for mom in range(4):
        rows = jnp.concatenate([screened_ref[128 * p + 32 * mom : 128 * p + 32 * mom + 32, :] for p in range(8)], axis=0)
        time_ref[mom] = jnp.dot(table, rows, preferred_element_type=jnp.float32)
    norm = 1.0 / math.sqrt(NK)
    own = own_ref[...].astype(jnp.float32)
    for step in (1, 2, 3, 0):
        if step == 0:
            moves[2].wait()
        for pair in range(2):
            at = 32 * step + 16 * pair
            tiles = [time_ref[k // 2, 128 * (k % 2) + at : 128 * (k % 2) + at + 16, :] * norm for k in range(NK)]
            cells = hartley8(tiles)
            for r in range(NK):
                at = 32 * (r % 2) + 16 * pair
                value = cell_refs[step][(r // 2) ^ mom_here, at : at + 16, :].astype(jnp.float32) * cells[r]
                sigma_ref[step, 64 * (r // 2) + at : 64 * (r // 2) + at + 16, :] = value.astype(jnp.bfloat16)
        if step == 1:
            for move in moves[:2]:
                move.wait()
        applied = jnp.dot(sigma_ref[step], coeffs_ref[...], preferred_element_type=jnp.float32)
        values = row_sums(applied.reshape(32, 8, NB) * own[None])
        for mom in range(4):
            for p in range(8):
                share = values[8 * mom : 8 * mom + 8, 128 * p : 128 * p + 128]
                out_ref[4 * mom + (tm_here ^ step), p] = share.astype(out_ref.dtype)


def row_sums(x):
    n = x.shape[-1]
    x = x.reshape(4, 8, 8, n)
    row = lax.broadcasted_iota(jnp.int32, (1, 1, 8, n), 2)
    turn = lambda v, by: pltpu.roll(v.reshape(-1, 8, n), by, 1).reshape(v.shape)
    for half in (4, 2, 1):
        low, high = x[:, :half], x[:, half:]
        x = jnp.where(row % (2 * half) < half, low + turn(low, 8 - half), high + turn(high, half))
    return x.reshape(32, n)


def start_all(copies, done):
    moves = [pltpu.make_async_copy(source, target, done.at[i]) for i, (source, target) in enumerate(copies)]
    for move in moves:
        move.start()
    return moves


def copy_all(copies, done):
    for move in start_all(copies, done):
        move.wait()


def split_times_kernel(place_ref, chi_ref, *refs):
    held, read, written = refs[4:]
    order = (3, 2, 1, 0)
    targets = [place_ref[1] ^ step for step in order]
    into = [refs[0] if step == 0 else held.at[step - 1] for step in order]
    reads = start_all([(chi_ref.at[:, target // 2, target % 2], to) for target, to in zip(targets, into)], read)
    writes = []
    for step, move in zip(order, reads):
        move.wait()
        if step:
            writes += start_all([(held.at[step - 1], refs[step])], written.at[pl.ds(step, 1)])
    for move in writes:
        move.wait()


def split_rows_kernel(place_ref, green_ref, *refs):
    held, read, written = refs[4:]
    starts = [jnp.minimum(4 * (place_ref[0] ^ step), GROUPS - 4) for step in range(4)]
    moves = start_all([(green_ref.at[:, pl.ds(start, 4)], held.at[step]) for step, start in enumerate(starts)], read)
    for step, move in enumerate(moves):
        move.wait()
        pltpu.make_async_copy(held.at[step], refs[step], written.at[step]).start()
    for step in range(4):
        pltpu.make_async_copy(held.at[step], refs[step], written.at[step]).wait()


def split_groups_kernel(place_ref, *refs):
    held, read, written = refs[8:]
    copy_all([(refs[part].at[:, place_ref[1] ^ step], held.at[step, part]) for step in range(4) for part in range(4)], read)
    copy_all([(held.at[step], refs[4 + step]) for step in range(4)], written)


def arrived_kernel(*refs):
    refs[-1][...] = jnp.zeros((8, 128), jnp.float32)


ANY = pl.BlockSpec(memory_space=pl.ANY)
SMEM = pl.BlockSpec(memory_space=pltpu.SMEM)
VMEM = pl.BlockSpec(memory_space=pltpu.VMEM)
HBM = pl.BlockSpec(memory_space=pltpu.HBM)


def in_hbm(array):
    return pltpu.with_memory_space_constraint(array, pltpu.HBM)


def in_vmem(array):
    return pltpu.with_memory_space_constraint(array, pltpu.VMEM)


def copies_call(kernel, outs, space, inputs, scratch, cost=None):
    return pl.pallas_call(
        kernel,
        out_shape=outs,
        in_specs=[SMEM] + [ANY] * inputs,
        out_specs=[space] * len(outs),
        scratch_shapes=scratch,
        compiler_params=pltpu.CompilerParams(vmem_limit_bytes=4 * MIB),
        cost_estimate=cost,
    )


def sems(count):
    return pltpu.SemaphoreType.DMA((count,))


def local(chi_time, green, band_coeffs):
    mom = lax.axis_index("mom")
    tm = lax.axis_index("zlo") * 2 + lax.axis_index("core")
    place = jnp.stack([mom, tm]).astype(jnp.int32)
    wide, narrow, back = [lax.dynamic_index_in_dim(jnp.asarray(tables), tm, 0, False) for tables in mixing_tables()]
    vmem = lambda mib: pltpu.CompilerParams(vmem_limit_bytes=mib * MIB)
    long = pl.CostEstimate(flops=100000000000, transcendentals=0, bytes_accessed=4 * MIB)

    quarter = (4, 56, NP)
    pieces = pl.pallas_call(
        split_times_kernel,
        out_shape=[jax.ShapeDtypeStruct(quarter, jnp.bfloat16)] + [pltpu.HBM(quarter, jnp.bfloat16)] * 3,
        in_specs=[SMEM, HBM],
        out_specs=[VMEM] + [HBM] * 3,
        scratch_shapes=[pltpu.VMEM((3, *quarter), jnp.bfloat16), sems(4), sems(4)],
        compiler_params=vmem(4),
    )(place, in_hbm(chi_time.reshape(4, 2, 2, 56, NP)))
    pieces = list(pieces)

    green, pieces[1] = lax.optimization_barrier((green, pieces[1]))
    parts = copies_call(
        split_rows_kernel,
        [pltpu.HBM((8, 4, 8, NP), jnp.bfloat16)] * 4,
        HBM,
        1,
        [pltpu.VMEM((4, 8, 4, 8, NP), jnp.bfloat16), sems(4), sems(4)],
        cost=long,
    )(place, in_hbm(green.reshape(8, GROUPS, 8, NP)))
    received = [pieces[0]] + [swap(pieces[step], TM, step) for step in (1, 2, 3)]
    by_mom = [parts[0]] + [swap(parts[step], "mom", step) for step in (1, 2, 3)]

    mixed = pl.pallas_call(
        frequency_kernel,
        out_shape=pltpu.HBM((NT, 56, NP), jnp.bfloat16),
        out_specs=HBM,
        scratch_shapes=[pltpu.VMEM((NT, 56, NP), jnp.bfloat16), sems(4)],
        compiler_params=vmem(8),
        cost_estimate=long,
    )(*received, wide, narrow)
    groups = copies_call(
        split_groups_kernel,
        [pltpu.HBM((4, 8, 8, NP), jnp.bfloat16)] * 4,
        HBM,
        4,
        [pltpu.VMEM((4, 4, 8, 8, NP), jnp.bfloat16), sems(16), sems(4)],
        cost=long,
    )(place, *by_mom)
    tile = exchange(mixed, PLANE).reshape(NP, NP)
    cells = [groups[0]] + [swap(groups[step], TM, step) for step in (1, 2, 3)]
    cells = [cell.reshape(4, 64, NP) for cell in cells]
    arrived = pl.pallas_call(
        arrived_kernel,
        out_shape=jax.ShapeDtypeStruct((8, 128), jnp.float32),
        in_specs=[VMEM] * 2,
        compiler_params=vmem(1),
        cost_estimate=long,
    )(*cells[2:])

    square = pltpu.VMEM((NP, NP), jnp.bfloat16)
    screened = pl.pallas_call(
        series_kernel,
        out_shape=pltpu.HBM((1024, NP), jnp.bfloat16),
        out_specs=HBM,
        scratch_shapes=[square, square, pltpu.VMEM((NP, NP), jnp.float32), square, square]
        + [pltpu.VMEM((1024, NP), jnp.bfloat16), sems(5)],
        compiler_params=vmem(16),
        cost_estimate=None,
    )(tile)
    spread = exchange(screened.reshape(128, 8, NP), BY_ROWS).reshape(1024, NP)

    group = jnp.minimum(4 * mom, GROUPS - 4) + tm
    row = (lax.axis_index("x") * 2 + lax.axis_index("zhi")) * 112 + 8 * group
    own = lax.dynamic_slice_in_dim(band_coeffs, row, 8, 0)
    partial_sums = pl.pallas_call(
        self_energy_kernel,
        out_shape=jax.ShapeDtypeStruct((16, 8, 8, 128), jnp.bfloat16),
        in_specs=[SMEM, VMEM, VMEM, HBM, VMEM, VMEM, VMEM, HBM, VMEM, HBM],
        scratch_shapes=[pltpu.VMEM((4, 256, NP), jnp.float32), pltpu.VMEM((4, 256, NP), jnp.bfloat16)]
        + [pltpu.VMEM((NP, NB), jnp.bfloat16), pltpu.VMEM((4, 64, NP), jnp.bfloat16), sems(3)],
        compiler_params=vmem(12),
    )(place, in_vmem(spread), back, in_hbm(cells[0]), *cells[1:], in_hbm(band_coeffs), own, in_hbm(arrived))
    shares = exchange(partial_sums.reshape(128, 8, 128), BY_OUTPUT)
    return shares.astype(jnp.float32).sum(axis=0).reshape(2, 4, 128)


def solution(mesh):
    fine = Mesh(mesh.devices.reshape(4, 2, 2, 4, 2), ("mom", "zlo", "core", "x", "zhi"))
    placed = (P(TM, "mom", ("x", "zhi"), None), P("mom", TM, ("x", "zhi"), None), P())
    return jax.shard_map(
        local, mesh=fine, in_specs=placed, out_specs=P("mom", TM, ("x", "zhi")), check_vma=False
    )
```

```python
import math

import jax
import jax.numpy as jnp
import ml_dtypes
import numpy as np
from jax import lax
from jax.experimental import pallas as pl
from jax.experimental.pallas import tpu as pltpu
from jax.sharding import Mesh
from jax.sharding import PartitionSpec as P

COUPLING = 0.8
NT, NK, NP, NB = 16, 8, 896, 1024
GROUPS = 14

C5 = (math.sqrt(22.0) - 1.0) / 4.0
C3 = 0.75 - C5
C4 = 0.625
C6 = 2.0 - 1.25 * C5

TM = ("zlo", "core")
PLANE = ("x", "zhi", "core")
BY_ROWS = ("x", "zhi", "mom", "zlo", "core")
BY_OUTPUT = ("mom", "zlo", "core", "x", "zhi")
MIB = 1024 * 1024


def exchange(pieces, axes):
    return lax.all_to_all(pieces, axes, split_axis=0, concat_axis=0, tiled=True)


def swap(piece, axes, step):
    return lax.ppermute(piece, axes, [(i, i ^ step) for i in range(4)])


def mixing_tables():
    index = np.arange(NT) + 0.5
    cosine = (np.sqrt(2.0 / NT) * np.cos(np.pi * index[:, None] * index[None, :] / NT)).astype(np.float32)
    wide, narrow, back = [], [], []
    for tm in range(4):
        times = [4 * ((place // 4) ^ tm) + place % 4 for place in range(NT)]
        wide.append(np.kron(cosine[:, times], np.eye(16)))
        narrow.append(np.kron(cosine[:, times], np.eye(8)))
        back.append(np.einsum("tpq,cd,ab->ctapdqb", cosine[times, :].reshape(NT, 8, 2), np.eye(2), np.eye(8)).reshape(256, 256))
    return [np.stack(tables).astype(ml_dtypes.bfloat16) for tables in (wide, narrow, back)]


def frequency_kernel(own_ref, first_ref, second_ref, third_ref, wide_ref, narrow_ref, out_ref, mixed_ref, sent):
    pieces = (own_ref, first_ref, second_ref, third_ref)
    scale = COUPLING / math.sqrt(NP)
    rows = jnp.concatenate([piece[t, 48:56, :].astype(jnp.float32) for piece in pieces for t in range(4)], axis=0)
    mixed = jnp.dot(narrow_ref[...], rows.astype(jnp.bfloat16), preferred_element_type=jnp.float32) * scale
    mixed_ref[:, 48:56, :] = mixed.reshape(NT, 8, NP).astype(jnp.bfloat16)
    moves = start_all([(mixed_ref.at[:, pl.ds(48, 8)], out_ref.at[:, pl.ds(48, 8)])], sent.at[pl.ds(0, 1)])
    for at in range(0, 48, 16):
        rows = jnp.concatenate([piece[t, at : at + 16, :] for piece in pieces for t in range(4)], axis=0)
        mixed = jnp.dot(wide_ref[...], rows, preferred_element_type=jnp.float32) * scale
        mixed_ref[:, at : at + 16, :] = mixed.reshape(NT, 16, NP).astype(jnp.bfloat16)
        moves += start_all([(mixed_ref.at[:, pl.ds(at, 16)], out_ref.at[:, pl.ds(at, 16)])], sent.at[pl.ds(1 + at // 16, 1)])
    for move in moves:
        move.wait()


def series_kernel(tile_ref, out_ref, square_ref, sum_ref, fourth_ref, left_ref, right_ref, padded_ref, sent):
    step = 448
    for at in range(0, NP, step):
        rows = slice(at, at + step)
        square = jnp.dot(tile_ref[rows, :], tile_ref[...], preferred_element_type=jnp.float32).astype(jnp.bfloat16)
        square_ref[rows, :] = square
        sum_ref[rows, :] = (square.astype(jnp.float32) + 0.5 * tile_ref[rows, :].astype(jnp.float32)).astype(jnp.bfloat16)
    for at in range(0, NP, step):
        rows = slice(at, at + step)
        fourth = jnp.dot(square_ref[rows, :], sum_ref[...], preferred_element_type=jnp.float32)
        square = square_ref[rows, :].astype(jnp.float32)
        tile = tile_ref[rows, :].astype(jnp.float32)
        left_ref[rows, :] = (fourth + C3 * square + C4 * tile).astype(jnp.bfloat16)
        right_ref[rows, :] = (fourth + C5 * square).astype(jnp.bfloat16)
        fourth_ref[rows, :] = C6 * fourth + square + tile
    sends = []
    for at, count in (0, 448), (448, 224), (672, 112), (784, 112):
        rows = slice(at, at + count)
        total = jnp.dot(left_ref[rows, :], right_ref[...], preferred_element_type=jnp.float32) + fourth_ref[rows, :]
        total = total.astype(jnp.bfloat16)
        for half in range(count // 112):
            to = 128 * (at // 112 + half)
            padded_ref[to : to + 96, :] = total[112 * half : 112 * half + 96]
            padded_ref[to + 96 : to + 112, :] = jnp.zeros((16, NP), jnp.bfloat16)
            padded_ref[to + 112 : to + 128, :] = total[112 * half + 96 : 112 * half + 112]
        rows = pl.ds(128 * (at // 112), 128 * (count // 112))
        sends.append(pltpu.make_async_copy(padded_ref.at[rows], out_ref.at[rows], sent.at[len(sends)]))
        sends[-1].start()
    for send in sends:
        send.wait()


def hartley8(x):
    root = math.sqrt(2.0)
    a0, a1, a2, a3 = x[0] + x[4], x[1] + x[5], x[2] + x[6], x[3] + x[7]
    b0, b1, b2, b3 = x[0] - x[4], x[1] - x[5], x[2] - x[6], x[3] - x[7]
    c0, c1, d0, d1 = a0 + a2, a1 + a3, a0 - a2, a1 - a3
    e0, e1, f1, f3 = b0 + b2, b0 - b2, root * b1, root * b3
    return [c0 + c1, e0 + f1, d0 + d1, e1 + f3, c0 - c1, e0 - f1, d0 - d1, e1 - f3]


def self_energy_kernel(place_ref, screened_ref, table_ref, *refs):
    cell_refs, (coeffs_hbm, own_ref, _, out_ref, time_ref, sigma_ref, coeffs_ref, held_ref, fetched) = list(refs[:4]), refs[4:]
    parts = [pl.ds(448 * i, 448) for i in range(2)]
    moves = start_all([(coeffs_hbm.at[part], coeffs_ref.at[part]) for part in parts] + [(cell_refs[0], held_ref)], fetched)
    cell_refs[0] = held_ref
    mom_here, tm_here = place_ref[0], place_ref[1]
    table = table_ref[...]
    for mom in range(4):
        rows = jnp.concatenate([screened_ref[128 * p + 32 * mom : 128 * p + 32 * mom + 32, :] for p in range(8)], axis=0)
        time_ref[mom] = jnp.dot(table, rows, preferred_element_type=jnp.float32)
    norm = 1.0 / math.sqrt(NK)
    own = own_ref[...].astype(jnp.float32)
    for step in (1, 2, 3, 0):
        if step == 0:
            moves[2].wait()
        for pair in range(2):
            at = 32 * step + 16 * pair
            tiles = [time_ref[k // 2, 128 * (k % 2) + at : 128 * (k % 2) + at + 16, :] * norm for k in range(NK)]
            cells = hartley8(tiles)
            for r in range(NK):
                at = 32 * (r % 2) + 16 * pair
                value = cell_refs[step][(r // 2) ^ mom_here, at : at + 16, :].astype(jnp.float32) * cells[r]
                sigma_ref[step, 64 * (r // 2) + at : 64 * (r // 2) + at + 16, :] = value.astype(jnp.bfloat16)
        if step == 1:
            for move in moves[:2]:
                move.wait()
        applied = jnp.dot(sigma_ref[step], coeffs_ref[...], preferred_element_type=jnp.float32)
        values = row_sums(applied.reshape(32, 8, NB) * own[None])
        for mom in range(4):
            for p in range(8):
                share = values[8 * mom : 8 * mom + 8, 128 * p : 128 * p + 128]
                out_ref[4 * mom + (tm_here ^ step), p] = share.astype(out_ref.dtype)


def row_sums(x):
    n = x.shape[-1]
    x = x.reshape(4, 8, 8, n)
    row = lax.broadcasted_iota(jnp.int32, (1, 1, 8, n), 2)
    turn = lambda v, by: pltpu.roll(v.reshape(-1, 8, n), by, 1).reshape(v.shape)
    for half in (4, 2, 1):
        low, high = x[:, :half], x[:, half:]
        x = jnp.where(row % (2 * half) < half, low + turn(low, 8 - half), high + turn(high, half))
    return x.reshape(32, n)


def start_all(copies, done):
    moves = [pltpu.make_async_copy(source, target, done.at[i]) for i, (source, target) in enumerate(copies)]
    for move in moves:
        move.start()
    return moves


def copy_all(copies, done):
    for move in start_all(copies, done):
        move.wait()


def split_times_kernel(place_ref, chi_ref, *refs):
    held, read, written = refs[4:]
    order = (3, 2, 1, 0)
    targets = [place_ref[1] ^ step for step in order]
    into = [refs[0] if step == 0 else held.at[step - 1] for step in order]
    reads = start_all([(chi_ref.at[:, target // 2, target % 2], to) for target, to in zip(targets, into)], read)
    writes = []
    for step, move in zip(order, reads):
        move.wait()
        if step:
            writes += start_all([(held.at[step - 1], refs[step])], written.at[pl.ds(step, 1)])
    for move in writes:
        move.wait()


def split_rows_kernel(place_ref, green_ref, *refs):
    held, read, written = refs[4:]
    starts = [jnp.minimum(4 * (place_ref[0] ^ step), GROUPS - 4) for step in range(4)]
    moves = start_all([(green_ref.at[:, pl.ds(start, 4)], held.at[step]) for step, start in enumerate(starts)], read)
    for step, move in enumerate(moves):
        move.wait()
        pltpu.make_async_copy(held.at[step], refs[step], written.at[step]).start()
    for step in range(4):
        pltpu.make_async_copy(held.at[step], refs[step], written.at[step]).wait()


def split_groups_kernel(place_ref, *refs):
    held, read, written = refs[8:]
    copy_all([(refs[part].at[:, place_ref[1] ^ step], held.at[step, part]) for step in range(4) for part in range(4)], read)
    copy_all([(held.at[step], refs[4 + step]) for step in range(4)], written)


def arrived_kernel(*refs):
    refs[-1][...] = jnp.zeros((8, 128), jnp.float32)


ANY = pl.BlockSpec(memory_space=pl.ANY)
SMEM = pl.BlockSpec(memory_space=pltpu.SMEM)
VMEM = pl.BlockSpec(memory_space=pltpu.VMEM)
HBM = pl.BlockSpec(memory_space=pltpu.HBM)


def in_hbm(array):
    return pltpu.with_memory_space_constraint(array, pltpu.HBM)


def in_vmem(array):
    return pltpu.with_memory_space_constraint(array, pltpu.VMEM)


def copies_call(kernel, outs, space, inputs, scratch, cost=None):
    return pl.pallas_call(
        kernel,
        out_shape=outs,
        in_specs=[SMEM] + [ANY] * inputs,
        out_specs=[space] * len(outs),
        scratch_shapes=scratch,
        compiler_params=pltpu.CompilerParams(vmem_limit_bytes=4 * MIB),
        cost_estimate=cost,
    )


def sems(count):
    return pltpu.SemaphoreType.DMA((count,))


def local(chi_time, green, band_coeffs):
    mom = lax.axis_index("mom")
    tm = lax.axis_index("zlo") * 2 + lax.axis_index("core")
    place = jnp.stack([mom, tm]).astype(jnp.int32)
    wide, narrow, back = [lax.dynamic_index_in_dim(jnp.asarray(tables), tm, 0, False) for tables in mixing_tables()]
    vmem = lambda mib: pltpu.CompilerParams(vmem_limit_bytes=mib * MIB)
    long = pl.CostEstimate(flops=100000000000, transcendentals=0, bytes_accessed=4 * MIB)

    quarter = (4, 56, NP)
    pieces = pl.pallas_call(
        split_times_kernel,
        out_shape=[jax.ShapeDtypeStruct(quarter, jnp.bfloat16)] + [pltpu.HBM(quarter, jnp.bfloat16)] * 3,
        in_specs=[SMEM, HBM],
        out_specs=[VMEM] + [HBM] * 3,
        scratch_shapes=[pltpu.VMEM((3, *quarter), jnp.bfloat16), sems(4), sems(4)],
        compiler_params=vmem(4),
    )(place, in_hbm(chi_time.reshape(4, 2, 2, 56, NP)))
    pieces = list(pieces)

    green, pieces[1] = lax.optimization_barrier((green, pieces[1]))
    parts = copies_call(
        split_rows_kernel,
        [pltpu.HBM((8, 4, 8, NP), jnp.bfloat16)] * 4,
        HBM,
        1,
        [pltpu.VMEM((4, 8, 4, 8, NP), jnp.bfloat16), sems(4), sems(4)],
        cost=long,
    )(place, in_hbm(green.reshape(8, GROUPS, 8, NP)))
    received = [pieces[0]] + [swap(pieces[step], TM, step) for step in (1, 2, 3)]
    by_mom = [parts[0]] + [swap(parts[step], "mom", step) for step in (1, 2, 3)]

    mixed = pl.pallas_call(
        frequency_kernel,
        out_shape=pltpu.HBM((NT, 56, NP), jnp.bfloat16),
        out_specs=HBM,
        scratch_shapes=[pltpu.VMEM((NT, 56, NP), jnp.bfloat16), sems(4)],
        compiler_params=vmem(8),
        cost_estimate=long,
    )(*received, wide, narrow)
    groups = copies_call(
        split_groups_kernel,
        [pltpu.HBM((4, 8, 8, NP), jnp.bfloat16)] * 4,
        HBM,
        4,
        [pltpu.VMEM((4, 4, 8, 8, NP), jnp.bfloat16), sems(16), sems(4)],
        cost=long,
    )(place, *by_mom)
    tile = exchange(mixed, PLANE).reshape(NP, NP)
    cells = [groups[0]] + [swap(groups[step], TM, step) for step in (1, 2, 3)]
    cells = [cell.reshape(4, 64, NP) for cell in cells]
    arrived = pl.pallas_call(
        arrived_kernel,
        out_shape=jax.ShapeDtypeStruct((8, 128), jnp.float32),
        in_specs=[VMEM] * 2,
        compiler_params=vmem(1),
        cost_estimate=long,
    )(*cells[2:])

    square = pltpu.VMEM((NP, NP), jnp.bfloat16)
    screened = pl.pallas_call(
        series_kernel,
        out_shape=pltpu.HBM((1024, NP), jnp.bfloat16),
        out_specs=HBM,
        scratch_shapes=[square, square, pltpu.VMEM((NP, NP), jnp.float32), square, square]
        + [pltpu.VMEM((1024, NP), jnp.bfloat16), sems(5)],
        compiler_params=vmem(22),
        cost_estimate=None,
    )(tile)
    spread = exchange(screened.reshape(128, 8, NP), BY_ROWS).reshape(1024, NP)

    group = jnp.minimum(4 * mom, GROUPS - 4) + tm
    row = (lax.axis_index("x") * 2 + lax.axis_index("zhi")) * 112 + 8 * group
    own = lax.dynamic_slice_in_dim(band_coeffs, row, 8, 0)
    partial_sums = pl.pallas_call(
        self_energy_kernel,
        out_shape=jax.ShapeDtypeStruct((16, 8, 8, 128), jnp.bfloat16),
        in_specs=[SMEM, VMEM, VMEM, HBM, VMEM, VMEM, VMEM, HBM, VMEM, HBM],
        scratch_shapes=[pltpu.VMEM((4, 256, NP), jnp.float32), pltpu.VMEM((4, 256, NP), jnp.bfloat16)]
        + [pltpu.VMEM((NP, NB), jnp.bfloat16), pltpu.VMEM((4, 64, NP), jnp.bfloat16), sems(3)],
        compiler_params=vmem(12),
    )(place, in_vmem(spread), back, in_hbm(cells[0]), *cells[1:], in_hbm(band_coeffs), own, in_hbm(arrived))
    shares = exchange(partial_sums.reshape(128, 8, 128), BY_OUTPUT)
    return shares.astype(jnp.float32).sum(axis=0).reshape(2, 4, 128)


def solution(mesh):
    fine = Mesh(mesh.devices.reshape(4, 2, 2, 4, 2), ("mom", "zlo", "core", "x", "zhi"))
    placed = (P(TM, "mom", ("x", "zhi"), None), P("mom", TM, ("x", "zhi"), None), P())
    return jax.shard_map(
        local, mesh=fine, in_specs=placed, out_specs=P("mom", TM, ("x", "zhi")), check_vma=False
    )
```
